128 devices in a mesh: row: 16 (over y, z), col: 8 (over x, core).
Axes of the slice: x: 4, y: 4, z: 4, core: 2. Of those that a mesh axis runs over, the one named last changes fastest.
Arguments:
- matrix: float32 [18432, 18432], P('row', 'col'), as said below
Outputs:
- updated: float32 [18432, 18432], P('row', 'col')
- reflectors: float32 [18432, 512], P('row')
Inputs may be any that keep to these rules, and one draw needn't show every extreme that they name: matrix is symmetric.
All inputs are finite; a program needn't handle non-finite values.
Results may differ from the reference program's by a relative error of at most 0.00016.
Values sent between devices are 32-bit elements; how exact they have to be, the bound alone decides.
A program may use at most 128 MiB of HBM per device.

```python
import jax
import jax.numpy as jnp
from jax import lax

NMAT = 18432
BAND = 256
PANELS = 2


def draw_matrix(key, part):
    first_key = jax.random.fold_in(key, 0)
    third_key = jax.random.fold_in(key, 2)
    random_part = jax.random.normal(first_key, (NMAT, NMAT), jnp.float32)
    planted = jax.random.normal(third_key, (2, BAND, BAND), jnp.float32)
    random_part = (random_part + random_part.T) * 0.7071
    planted = (planted + jnp.swapaxes(planted, 1, 2)) * 0.7071
    strength = 0.8 * jnp.sqrt(jnp.float32(NMAT))
    spread = 0.4 / jnp.sqrt(jnp.float32(BAND))
    unit_block = jnp.eye(BAND, dtype=jnp.float32)
    first_block = strength * (unit_block + spread * planted[0])
    second_block = -strength * (unit_block + spread * planted[1])
    empty_block = jnp.zeros((BAND, BAND), jnp.float32)
    upper_rows = jnp.concatenate([empty_block, first_block, empty_block], axis=1)
    middle_rows = jnp.concatenate([first_block, empty_block, second_block], axis=1)
    lower_rows = jnp.concatenate([empty_block, second_block, empty_block], axis=1)
    corner = jnp.concatenate([upper_rows, middle_rows, lower_rows], axis=0)
    rest = NMAT - 3 * BAND
    placed = jnp.pad(corner, ((0, rest), (0, rest)))
    return (random_part + placed).astype(jnp.float32)


def setup_inputs(seed: int = 0) -> dict:
    key_of = jax.random.split(jax.random.key(seed), 2)
    return {
        "matrix": draw_matrix(jax.random.fold_in(key_of[1], 71), 0),
    }


def reference(matrix):
    current = matrix
    positions = jnp.arange(NMAT, dtype=jnp.int32)
    columns = jnp.arange(BAND, dtype=jnp.int32)
    identity = jnp.eye(BAND, dtype=jnp.float32)
    high = lax.Precision.HIGHEST
    stored = []
    for which_panel in range(PANELS):
        start = (which_panel + 1) * BAND
        panel_rows = jnp.where(positions[:, None] >= start, current[:, which_panel * BAND:(which_panel + 1) * BAND], 0.0)
        unit_rows = (positions[:, None] - start == columns[None, :]).astype(jnp.float32)
        gram_sum = jnp.dot(panel_rows.T, panel_rows, precision=high)
        top_block = jnp.dot(unit_rows.T, panel_rows, precision=high)
        factor_low = jnp.linalg.cholesky(gram_sum)
        q_rows = jax.scipy.linalg.solve_triangular(factor_low, panel_rows.T, lower=True).T
        q_top = jax.scipy.linalg.solve_triangular(factor_low, top_block.T, lower=True).T
        shifted = identity + q_top
        factor_two = jnp.linalg.cholesky(jnp.dot(shifted, shifted.T, precision=high))
        inner = jax.scipy.linalg.solve_triangular(factor_two, identity, lower=True)
        transform = jnp.dot(shifted.T, jnp.dot(inner.T, inner, precision=high), precision=high)
        vectors = q_rows + unit_rows
        stored.append(vectors)
        image = jnp.dot(current, vectors, precision=high)
        curvature = jnp.dot(vectors.T, image, precision=high)
        middle = jnp.dot(jnp.dot(transform, curvature, precision=high), transform.T, precision=high)
        w_full = jnp.dot(image, transform.T, precision=high) - 0.5 * jnp.dot(vectors, middle, precision=high)
        current = current - jnp.dot(vectors, w_full.T, precision=high) - jnp.dot(w_full, vectors.T, precision=high)
    return (current, jnp.concatenate(stored, axis=1))
```

```python
import jax
import jax.numpy as jnp
from jax import lax
from jax.sharding import PartitionSpec as P

BAND = 256
PANELS = 2
HIGH = lax.Precision.HIGHEST


def mm(a, b):
    return jnp.dot(a, b, precision=HIGH)


def mm_tn(a, b):
    return lax.dot_general(a, b, (((0,), (0,)), ((), ())), precision=HIGH)


def mm_nt(a, b):
    return lax.dot_general(a, b, (((1,), (1,)), ((), ())), precision=HIGH)


def transpose_exchange(x, rows, cols):
    both = ("row", "col")
    first = []
    second = []
    for s in range(rows):
        for j in range(cols):
            src = s * cols + j
            first.append((src, (2 * j + s % 2) * cols + s // 2))
            second.append((src, (2 * j + 1 - s % 2) * cols + s // 2))
    got1 = lax.ppermute(x, both, first)
    got2 = lax.ppermute(x, both, second)
    odd_row = lax.axis_index("row") % 2 == 1
    even = jnp.where(odd_row, got2, got1)
    odd = jnp.where(odd_row, got1, got2)
    return jnp.concatenate([even, odd], axis=0)


def small_factors(gram, top):
    identity = jnp.eye(BAND, dtype=jnp.float32)
    low = jnp.linalg.cholesky(gram)
    low_inv = jax.scipy.linalg.solve_triangular(low, identity, lower=True)
    shifted = identity + mm_nt(top, low_inv)
    second = jnp.linalg.cholesky(mm_nt(shifted, shifted))
    second_inv = jax.scipy.linalg.solve_triangular(second, identity, lower=True)
    transform = mm_tn(shifted, mm_tn(second_inv, second_inv))
    return low_inv, transform


def body(a):
    rows = lax.psum(1, "row")
    cols = lax.psum(1, "col")
    row_count, col_count = a.shape
    r = lax.axis_index("row")
    c = lax.axis_index("col")
    row_pos = r * row_count + jnp.arange(row_count, dtype=jnp.int32)
    col_pos = c * col_count + jnp.arange(col_count, dtype=jnp.int32)
    band_idx = jnp.arange(BAND, dtype=jnp.int32)
    width = PANELS * BAND

    col_zero = c == 0
    colb = lax.psum(jnp.where(col_zero, a[:, :width], 0.0), "col")
    strip_t = transpose_exchange(colb, rows, cols)

    lo = BAND
    p0_loc = jnp.where(row_pos[:, None] >= lo, a[:, :BAND], 0.0)
    g_loc = jnp.where(col_zero, mm_tn(p0_loc, p0_loc), 0.0)
    top_loc = jnp.where(col_zero & (r == 0), a[lo:lo + BAND, :BAND], 0.0)
    gram0, top0 = lax.psum((g_loc, top_loc), ("row", "col"))

    stored = []
    current = a
    prev = None
    for k in range(PANELS):
        lo = (k + 1) * BAND
        if k == 0:
            gram, top = gram0, top0
            pr = jnp.where(row_pos[:, None] >= lo, colb[:, :BAND], 0.0)
            pc = jnp.where(col_pos[:, None] >= lo, strip_t[:, :BAND], 0.0)
        else:
            y_r0, w_r0, y_c0, w_c0, y_e0, w_e0 = prev
            pr = colb[:, k * BAND:(k + 1) * BAND] - mm_nt(y_r0, w_e0) - mm_nt(w_r0, y_e0)
            pc = strip_t[:, k * BAND:(k + 1) * BAND] - mm_nt(y_c0, w_e0) - mm_nt(w_c0, y_e0)
            pr = jnp.where(row_pos[:, None] >= lo, pr, 0.0)
            pc = jnp.where(col_pos[:, None] >= lo, pc, 0.0)
            g_part = mm_tn(pc, pc)
            top_part = jnp.where(col_zero, pc[lo:lo + BAND], 0.0)
            gram, top = lax.psum((g_part, top_part), "col")
        low_inv, transform = small_factors(gram, top)
        unit_r = (row_pos[:, None] - lo == band_idx[None, :]).astype(jnp.float32)
        unit_c = (col_pos[:, None] - lo == band_idx[None, :]).astype(jnp.float32)
        y_r = mm_nt(pr, low_inv) + unit_r
        y_c = mm_nt(pc, low_inv) + unit_c
        stored.append(y_r)

        xp = mm(current, y_c)
        if k + 1 < PANELS:
            nlo = (k + 1) * BAND
            ext = mm_tn(strip_t[:, nlo:nlo + BAND], y_c)
            x_r, x_e = lax.psum((xp, ext), "col")
        else:
            x_r = lax.psum(xp, "col")
        curv = lax.psum(mm_tn(y_r, xp), ("row", "col"))
        x_c = transpose_exchange(x_r, rows, cols)
        middle = mm_nt(mm(transform, curv), transform)
        w_r = mm_nt(x_r, transform) - 0.5 * mm(y_r, middle)
        w_c = mm_nt(x_c, transform) - 0.5 * mm(y_c, middle)
        current = current - mm_nt(y_r, w_c) - mm_nt(w_r, y_c)
        if k + 1 < PANELS:
            y_e = mm_nt(top, low_inv) + jnp.eye(BAND, dtype=jnp.float32)
            w_e = mm_nt(x_e, transform) - 0.5 * mm(y_e, middle)
            prev = (y_r, w_r, y_c, w_c, y_e, w_e)
    return current, jnp.concatenate(stored, axis=1)


def solution(mesh):
    return jax.shard_map(
        body,
        mesh=mesh,
        in_specs=(P("row", "col"),),
        out_specs=(P("row", "col"), P("row", None)),
        check_vma=False,
    )
```

```python
import functools
import itertools

import jax
import jax.numpy as jnp
from jax import lax
from jax.experimental import pallas as pl
from jax.experimental.pallas import tpu as pltpu
from jax.sharding import PartitionSpec as P

BAND = 256
PANELS = 2
HIGH = lax.Precision.HIGHEST
MESH_ID = pl.DeviceIdType.MESH


def mm(a, b):
    return jnp.dot(a, b, precision=HIGH)


def mm_tn(a, b):
    return lax.dot_general(a, b, (((0,), (0,)), ((), ())), precision=HIGH)


def mm_nt(a, b):
    return lax.dot_general(a, b, (((1,), (1,)), ((), ())), precision=HIGH)


def _a2a_kernel(axis, groups, x_ref, o_ref, local_sem, send_sems, recv_sems):
    me = lax.axis_index(axis)
    barrier = pltpu.get_barrier_semaphore()
    for k in range(1, groups):
        peer = (me + k) % groups
        pl.semaphore_signal(barrier, 1, device_id={axis: peer}, device_id_type=MESH_ID)
    pl.semaphore_wait(barrier, groups - 1)
    local = pltpu.make_async_copy(x_ref.at[me], o_ref.at[me], local_sem)
    local.start()
    copies = []
    for k in range(1, groups):
        peer = (me + k) % groups
        copy = pltpu.make_async_remote_copy(
            src_ref=x_ref.at[peer],
            dst_ref=o_ref.at[me],
            send_sem=send_sems.at[k],
            recv_sem=recv_sems.at[k],
            device_id={axis: peer},
            device_id_type=MESH_ID,
        )
        copy.start()
        copies.append(copy)
    for copy in copies:
        copy.wait_send()
    for copy in copies:
        copy.wait_recv()
    local.wait()


class Comm:
    def __init__(self):
        self.ids = itertools.count()

    def a2a(self, x, axis):
        groups = x.shape[0]
        return pl.pallas_call(
            functools.partial(_a2a_kernel, axis, groups),
            out_shape=jax.ShapeDtypeStruct(x.shape, x.dtype),
            in_specs=[pl.BlockSpec(memory_space=pl.ANY)],
            out_specs=pl.BlockSpec(memory_space=pl.ANY),
            scratch_shapes=[
                pltpu.SemaphoreType.DMA,
                pltpu.SemaphoreType.DMA((groups,)),
                pltpu.SemaphoreType.DMA((groups,)),
            ],
            compiler_params=pltpu.CompilerParams(
                collective_id=next(self.ids), has_side_effects=True
            ),
        )(x)

    def reduce_scatter(self, x, axis, groups):
        parts = self.a2a(x.reshape(groups, x.shape[0] // groups, *x.shape[1:]), axis)
        return jnp.sum(parts, axis=0)

    def all_gather(self, x, axis, groups):
        got = self.a2a(jnp.broadcast_to(x[None], (groups,) + x.shape), axis)
        return got.reshape(groups * x.shape[0], *x.shape[1:])

    def psum(self, x, axis, groups):
        return self.all_gather(self.reduce_scatter(x, axis, groups), axis, groups)

    def broadcast(self, x, axis, groups, root):
        parts = self.a2a(x.reshape(groups, x.shape[0] // groups, *x.shape[1:]), axis)
        return self.all_gather(parts[root], axis, groups)


def transpose_exchange(x, rows, cols):
    both = ("row", "col")
    first = []
    second = []
    for s in range(rows):
        for j in range(cols):
            src = s * cols + j
            first.append((src, (2 * j + s % 2) * cols + s // 2))
            second.append((src, (2 * j + 1 - s % 2) * cols + s // 2))
    got1 = lax.ppermute(x, both, first)
    got2 = lax.ppermute(x, both, second)
    odd_row = lax.axis_index("row") % 2 == 1
    even = jnp.where(odd_row, got2, got1)
    odd = jnp.where(odd_row, got1, got2)
    return jnp.concatenate([even, odd], axis=0)


def small_factors(gram, top):
    identity = jnp.eye(BAND, dtype=jnp.float32)
    low = jnp.linalg.cholesky(gram)
    low_inv = jax.scipy.linalg.solve_triangular(low, identity, lower=True)
    shifted = identity + mm_nt(top, low_inv)
    second = jnp.linalg.cholesky(mm_nt(shifted, shifted))
    second_inv = jax.scipy.linalg.solve_triangular(second, identity, lower=True)
    transform = mm_tn(shifted, mm_tn(second_inv, second_inv))
    return low_inv, transform


def body(a):
    comm = Comm()
    rows = lax.psum(1, "row")
    cols = lax.psum(1, "col")
    row_count, col_count = a.shape
    r = lax.axis_index("row")
    c = lax.axis_index("col")
    row_pos = r * row_count + jnp.arange(row_count, dtype=jnp.int32)
    col_pos = c * col_count + jnp.arange(col_count, dtype=jnp.int32)
    band_idx = jnp.arange(BAND, dtype=jnp.int32)
    width = PANELS * BAND

    colb = comm.broadcast(a[:, :width], "col", cols, 0)
    lo = BAND
    p0 = jnp.where(row_pos[:, None] >= lo, colb[:, :BAND], 0.0)
    top_part = jnp.where(r == 0, colb[lo:lo + BAND, :BAND], 0.0)
    summed = comm.psum(jnp.concatenate([mm_tn(p0, p0), top_part], axis=0), "row", rows)
    gram0, top0 = summed[:BAND], summed[BAND:]
    strip_t = transpose_exchange(colb, rows, cols)

    stored = []
    current = a
    prev = None
    for k in range(PANELS):
        lo = (k + 1) * BAND
        if k == 0:
            gram, top = gram0, top0
            pr = p0
            pc = jnp.where(col_pos[:, None] >= lo, strip_t[:, :BAND], 0.0)
        else:
            y_r0, w_r0, y_c0, w_c0, y_e0, w_e0 = prev
            pr = colb[:, k * BAND:(k + 1) * BAND] - mm_nt(y_r0, w_e0) - mm_nt(w_r0, y_e0)
            pc = strip_t[:, k * BAND:(k + 1) * BAND] - mm_nt(y_c0, w_e0) - mm_nt(w_c0, y_e0)
            pr = jnp.where(row_pos[:, None] >= lo, pr, 0.0)
            pc = jnp.where(col_pos[:, None] >= lo, pc, 0.0)
            top_part = jnp.where(c == 0, pc[lo:lo + BAND], 0.0)
            summed = comm.psum(jnp.concatenate([mm_tn(pc, pc), top_part], axis=0), "col", cols)
            gram, top = summed[:BAND], summed[BAND:]
        low_inv, transform = small_factors(gram, top)
        unit_r = (row_pos[:, None] - lo == band_idx[None, :]).astype(jnp.float32)
        unit_c = (col_pos[:, None] - lo == band_idx[None, :]).astype(jnp.float32)
        y_r = mm_nt(pr, low_inv) + unit_r
        y_c = mm_nt(pc, low_inv) + unit_c
        stored.append(y_r)

        xp = mm(current, y_c)
        parts = [xp, mm_tn(y_r, xp)]
        if k + 1 < PANELS:
            nlo = (k + 1) * BAND
            parts.append(mm_tn(strip_t[:, nlo:nlo + BAND], y_c))
        summed = comm.psum(jnp.concatenate(parts, axis=0), "col", cols)
        x_r = summed[:row_count]
        curv = comm.psum(summed[row_count:row_count + BAND], "row", rows)
        x_c = transpose_exchange(x_r, rows, cols)
        middle = mm_nt(mm(transform, curv), transform)
        w_r = mm_nt(x_r, transform) - 0.5 * mm(y_r, middle)
        w_c = mm_nt(x_c, transform) - 0.5 * mm(y_c, middle)
        current = current - mm_nt(y_r, w_c) - mm_nt(w_r, y_c)
        if k + 1 < PANELS:
            x_e = summed[row_count + BAND:]
            y_e = mm_nt(top, low_inv) + jnp.eye(BAND, dtype=jnp.float32)
            w_e = mm_nt(x_e, transform) - 0.5 * mm(y_e, middle)
            prev = (y_r, w_r, y_c, w_c, y_e, w_e)
    return current, jnp.concatenate(stored, axis=1)


def solution(mesh):
    return jax.shard_map(
        body,
        mesh=mesh,
        in_specs=(P("row", "col"),),
        out_specs=(P("row", "col"), P("row", None)),
        check_vma=False,
    )
```

```python
import functools
import itertools

import jax
import jax.numpy as jnp
from jax import lax
from jax.experimental import pallas as pl
from jax.experimental.pallas import tpu as pltpu
from jax.sharding import PartitionSpec as P

BAND = 256
PANELS = 2
HIGH = lax.Precision.HIGHEST
FAST = lax.Precision.HIGH
MESH_ID = pl.DeviceIdType.MESH


def mm(a, b, precision=HIGH):
    return jnp.dot(a, b, precision=precision)


def mm_tn(a, b, precision=HIGH):
    return lax.dot_general(a, b, (((0,), (0,)), ((), ())), precision=precision)


def mm_nt(a, b, precision=HIGH):
    return lax.dot_general(a, b, (((1,), (1,)), ((), ())), precision=precision)


def _a2a_kernel(axis, groups, x_ref, o_ref, local_sem, send_sems, recv_sems):
    me = lax.axis_index(axis)
    barrier = pltpu.get_barrier_semaphore()
    for k in range(1, groups):
        peer = (me + k) % groups
        pl.semaphore_signal(barrier, 1, device_id={axis: peer}, device_id_type=MESH_ID)
    pl.semaphore_wait(barrier, groups - 1)
    local = pltpu.make_async_copy(x_ref.at[me], o_ref.at[me], local_sem)
    local.start()
    copies = []
    for k in range(1, groups):
        peer = (me + k) % groups
        copy = pltpu.make_async_remote_copy(
            src_ref=x_ref.at[peer],
            dst_ref=o_ref.at[me],
            send_sem=send_sems.at[k],
            recv_sem=recv_sems.at[k],
            device_id={axis: peer},
            device_id_type=MESH_ID,
        )
        copy.start()
        copies.append(copy)
    for copy in copies:
        copy.wait_send()
    for copy in copies:
        copy.wait_recv()
    local.wait()


class Comm:
    def __init__(self):
        self.ids = itertools.count()

    def a2a(self, x, axis):
        groups = x.shape[0]
        return pl.pallas_call(
            functools.partial(_a2a_kernel, axis, groups),
            out_shape=jax.ShapeDtypeStruct(x.shape, x.dtype),
            in_specs=[pl.BlockSpec(memory_space=pl.ANY)],
            out_specs=pl.BlockSpec(memory_space=pl.ANY),
            scratch_shapes=[
                pltpu.SemaphoreType.DMA,
                pltpu.SemaphoreType.DMA((groups,)),
                pltpu.SemaphoreType.DMA((groups,)),
            ],
            compiler_params=pltpu.CompilerParams(
                collective_id=next(self.ids), has_side_effects=True
            ),
        )(x)

    def reduce_scatter(self, x, axis, groups):
        parts = self.a2a(x.reshape(groups, x.shape[0] // groups, *x.shape[1:]), axis)
        return jnp.sum(parts, axis=0)

    def all_gather(self, x, axis, groups):
        got = self.a2a(jnp.broadcast_to(x[None], (groups,) + x.shape), axis)
        return got.reshape(groups * x.shape[0], *x.shape[1:])

    def psum(self, x, axis, groups):
        return self.all_gather(self.reduce_scatter(x, axis, groups), axis, groups)

    def broadcast(self, x, axis, groups, root):
        parts = self.a2a(x.reshape(groups, x.shape[0] // groups, *x.shape[1:]), axis)
        return self.all_gather(parts[root], axis, groups)


def transpose_exchange(x, rows, cols):
    both = ("row", "col")
    first = []
    second = []
    for s in range(rows):
        for j in range(cols):
            src = s * cols + j
            first.append((src, (2 * j + s % 2) * cols + s // 2))
            second.append((src, (2 * j + 1 - s % 2) * cols + s // 2))
    got1 = lax.ppermute(x, both, first)
    got2 = lax.ppermute(x, both, second)
    odd_row = lax.axis_index("row") % 2 == 1
    even = jnp.where(odd_row, got2, got1)
    odd = jnp.where(odd_row, got1, got2)
    return jnp.concatenate([even, odd], axis=0)


def small_factors(gram, top):
    identity = jnp.eye(BAND, dtype=jnp.float32)
    low = jnp.linalg.cholesky(gram)
    low_inv = jax.scipy.linalg.solve_triangular(low, identity, lower=True)
    shifted = identity + mm_nt(top, low_inv)
    second = jnp.linalg.cholesky(mm_nt(shifted, shifted))
    second_inv = jax.scipy.linalg.solve_triangular(second, identity, lower=True)
    transform = mm_tn(shifted, mm_tn(second_inv, second_inv))
    return low_inv, transform


def body(a):
    comm = Comm()
    rows = lax.psum(1, "row")
    cols = lax.psum(1, "col")
    row_count, col_count = a.shape
    r = lax.axis_index("row")
    c = lax.axis_index("col")
    row_pos = r * row_count + jnp.arange(row_count, dtype=jnp.int32)
    col_pos = c * col_count + jnp.arange(col_count, dtype=jnp.int32)
    band_idx = jnp.arange(BAND, dtype=jnp.int32)
    width = PANELS * BAND

    colb = comm.broadcast(a[:, :width], "col", cols, 0)
    lo = BAND
    p0 = jnp.where(row_pos[:, None] >= lo, colb[:, :BAND], 0.0)
    top_part = jnp.where(r == 0, colb[lo:lo + BAND, :BAND], 0.0)
    summed = comm.psum(jnp.concatenate([mm_tn(p0, p0), top_part], axis=0), "row", rows)
    gram0, top0 = summed[:BAND], summed[BAND:]
    strip_t = transpose_exchange(colb, rows, cols)

    stored = []
    current = a
    prev = None
    for k in range(PANELS):
        lo = (k + 1) * BAND
        if k == 0:
            gram, top = gram0, top0
            pr = p0
            pc = jnp.where(col_pos[:, None] >= lo, strip_t[:, :BAND], 0.0)
        else:
            y_r0, w_r0, y_c0, w_c0, y_e0, w_e0 = prev
            pr = colb[:, k * BAND:(k + 1) * BAND] - mm_nt(y_r0, w_e0) - mm_nt(w_r0, y_e0)
            pc = strip_t[:, k * BAND:(k + 1) * BAND] - mm_nt(y_c0, w_e0) - mm_nt(w_c0, y_e0)
            pr = jnp.where(row_pos[:, None] >= lo, pr, 0.0)
            pc = jnp.where(col_pos[:, None] >= lo, pc, 0.0)
            top_part = jnp.where(c == 0, pc[lo:lo + BAND], 0.0)
            summed = comm.psum(jnp.concatenate([mm_tn(pc, pc), top_part], axis=0), "col", cols)
            gram, top = summed[:BAND], summed[BAND:]
        low_inv, transform = small_factors(gram, top)
        unit_r = (row_pos[:, None] - lo == band_idx[None, :]).astype(jnp.float32)
        unit_c = (col_pos[:, None] - lo == band_idx[None, :]).astype(jnp.float32)
        y_r = mm_nt(pr, low_inv) + unit_r
        y_c = mm_nt(pc, low_inv) + unit_c
        stored.append(y_r)

        xp = mm(current, y_c, FAST)
        xq = mm_tn(current, y_r, FAST)
        summed_c = comm.psum(jnp.concatenate([xq, mm_tn(y_r, xp)], axis=0), "row", rows)
        x_c = summed_c[:col_count]
        parts = [xp, summed_c[col_count:]]
        if k + 1 < PANELS:
            nlo = (k + 1) * BAND
            parts.append(mm_tn(strip_t[:, nlo:nlo + BAND], y_c))
        summed = comm.psum(jnp.concatenate(parts, axis=0), "col", cols)
        x_r = summed[:row_count]
        curv = summed[row_count:row_count + BAND]
        middle = mm_nt(mm(transform, curv), transform)
        w_r = mm_nt(x_r, transform) - 0.5 * mm(y_r, middle)
        w_c = mm_nt(x_c, transform) - 0.5 * mm(y_c, middle)
        current = current - mm_nt(y_r, w_c, FAST) - mm_nt(w_r, y_c, FAST)
        if k + 1 < PANELS:
            x_e = summed[row_count + BAND:]
            y_e = mm_nt(top, low_inv) + jnp.eye(BAND, dtype=jnp.float32)
            w_e = mm_nt(x_e, transform) - 0.5 * mm(y_e, middle)
            prev = (y_r, w_r, y_c, w_c, y_e, w_e)
    return current, jnp.concatenate(stored, axis=1)


def solution(mesh):
    return jax.shard_map(
        body,
        mesh=mesh,
        in_specs=(P("row", "col"),),
        out_specs=(P("row", "col"), P("row", None)),
        check_vma=False,
    )
```

```python
import jax
import jax.numpy as jnp
from jax import lax
from jax.sharding import PartitionSpec as P

BAND = 256
PANELS = 2
HIGH = lax.Precision.HIGHEST
FAST = lax.Precision.HIGH


def mm(a, b, precision=HIGH):
    return jnp.dot(a, b, precision=precision)


def mm_tn(a, b, precision=HIGH):
    return lax.dot_general(a, b, (((0,), (0,)), ((), ())), precision=precision)


def mm_nt(a, b, precision=HIGH):
    return lax.dot_general(a, b, (((1,), (1,)), ((), ())), precision=precision)


class Comm:
    def a2a(self, x, axis):
        return lax.all_to_all(x, axis, 0, 0, tiled=False)

    def reduce_scatter(self, x, axis, groups):
        parts = self.a2a(x.reshape(groups, x.shape[0] // groups, *x.shape[1:]), axis)
        return jnp.sum(parts, axis=0)

    def all_gather(self, x, axis, groups):
        got = self.a2a(jnp.broadcast_to(x[None], (groups,) + x.shape), axis)
        return got.reshape(groups * x.shape[0], *x.shape[1:])

    def psum(self, x, axis, groups):
        return self.all_gather(self.reduce_scatter(x, axis, groups), axis, groups)

    def broadcast(self, x, axis, groups, root):
        parts = self.a2a(x.reshape(groups, x.shape[0] // groups, *x.shape[1:]), axis)
        return self.all_gather(parts[root], axis, groups)


def transpose_exchange(x, rows, cols):
    both = ("row", "col")
    first = []
    second = []
    for s in range(rows):
        for j in range(cols):
            src = s * cols + j
            first.append((src, (2 * j + s % 2) * cols + s // 2))
            second.append((src, (2 * j + 1 - s % 2) * cols + s // 2))
    got1 = lax.ppermute(x, both, first)
    got2 = lax.ppermute(x, both, second)
    odd_row = lax.axis_index("row") % 2 == 1
    even = jnp.where(odd_row, got2, got1)
    odd = jnp.where(odd_row, got1, got2)
    return jnp.concatenate([even, odd], axis=0)


def small_factors(gram, top):
    identity = jnp.eye(BAND, dtype=jnp.float32)
    low = jnp.linalg.cholesky(gram)
    low_inv = jax.scipy.linalg.solve_triangular(low, identity, lower=True)
    shifted = identity + mm_nt(top, low_inv)
    second = jnp.linalg.cholesky(mm_nt(shifted, shifted))
    second_inv = jax.scipy.linalg.solve_triangular(second, identity, lower=True)
    transform = mm_tn(shifted, mm_tn(second_inv, second_inv))
    return low_inv, transform


def body(a):
    comm = Comm()
    rows = lax.psum(1, "row")
    cols = lax.psum(1, "col")
    row_count, col_count = a.shape
    r = lax.axis_index("row")
    c = lax.axis_index("col")
    row_pos = r * row_count + jnp.arange(row_count, dtype=jnp.int32)
    col_pos = c * col_count + jnp.arange(col_count, dtype=jnp.int32)
    band_idx = jnp.arange(BAND, dtype=jnp.int32)
    width = PANELS * BAND

    colb = comm.broadcast(a[:, :width], "col", cols, 0)
    lo = BAND
    p0 = jnp.where(row_pos[:, None] >= lo, colb[:, :BAND], 0.0)
    top_part = jnp.where(r == 0, colb[lo:lo + BAND, :BAND], 0.0)
    summed = comm.psum(jnp.concatenate([mm_tn(p0, p0), top_part], axis=0), "row", rows)
    gram0, top0 = summed[:BAND], summed[BAND:]
    colb_late, summed = lax.optimization_barrier((colb, summed))
    gram0, top0 = summed[:BAND], summed[BAND:]
    strip_t = transpose_exchange(colb_late, rows, cols)

    stored = []
    current = a
    prev = None
    for k in range(PANELS):
        lo = (k + 1) * BAND
        if k == 0:
            gram, top = gram0, top0
            pr = p0
            pc = jnp.where(col_pos[:, None] >= lo, strip_t[:, :BAND], 0.0)
        else:
            y_r0, w_r0, y_c0, w_c0, y_e0, w_e0 = prev
            pr = colb[:, k * BAND:(k + 1) * BAND] - mm_nt(y_r0, w_e0) - mm_nt(w_r0, y_e0)
            pc = strip_t[:, k * BAND:(k + 1) * BAND] - mm_nt(y_c0, w_e0) - mm_nt(w_c0, y_e0)
            pr = jnp.where(row_pos[:, None] >= lo, pr, 0.0)
            pc = jnp.where(col_pos[:, None] >= lo, pc, 0.0)
            top_part = jnp.where(c == 0, pc[lo:lo + BAND], 0.0)
            summed = comm.psum(jnp.concatenate([mm_tn(pc, pc), top_part], axis=0), "col", cols)
            gram, top = summed[:BAND], summed[BAND:]
        low_inv, transform = small_factors(gram, top)
        unit_r = (row_pos[:, None] - lo == band_idx[None, :]).astype(jnp.float32)
        unit_c = (col_pos[:, None] - lo == band_idx[None, :]).astype(jnp.float32)
        y_r = mm_nt(pr, low_inv) + unit_r
        y_c = mm_nt(pc, low_inv) + unit_c
        stored.append(y_r)

        xp = mm(current, y_c, FAST)
        xq = mm_tn(current, y_r, FAST)
        summed_c = comm.psum(jnp.concatenate([xq, mm_tn(y_r, xp)], axis=0), "row", rows)
        x_c = summed_c[:col_count]
        parts = [xp, summed_c[col_count:]]
        if k + 1 < PANELS:
            nlo = (k + 1) * BAND
            parts.append(mm_tn(strip_t[:, nlo:nlo + BAND], y_c))
        summed = comm.psum(jnp.concatenate(parts, axis=0), "col", cols)
        x_r = summed[:row_count]
        curv = summed[row_count:row_count + BAND]
        middle = mm_nt(mm(transform, curv), transform)
        w_r = mm_nt(x_r, transform) - 0.5 * mm(y_r, middle)
        w_c = mm_nt(x_c, transform) - 0.5 * mm(y_c, middle)
        current = current - mm_nt(y_r, w_c, FAST) - mm_nt(w_r, y_c, FAST)
        if k + 1 < PANELS:
            x_e = summed[row_count + BAND:]
            y_e = mm_nt(top, low_inv) + jnp.eye(BAND, dtype=jnp.float32)
            w_e = mm_nt(x_e, transform) - 0.5 * mm(y_e, middle)
            prev = (y_r, w_r, y_c, w_c, y_e, w_e)
    return current, jnp.concatenate(stored, axis=1)


def solution(mesh):
    return jax.shard_map(
        body,
        mesh=mesh,
        in_specs=(P("row", "col"),),
        out_specs=(P("row", "col"), P("row", None)),
        check_vma=False,
    )
```

```python
import jax
import jax.numpy as jnp
from jax import lax
from jax.sharding import PartitionSpec as P

BAND = 256
PANELS = 2
HIGH = lax.Precision.HIGHEST
FAST = lax.Precision.HIGH


def mm(a, b, precision=HIGH):
    return jnp.dot(a, b, precision=precision)


def mm_tn(a, b, precision=HIGH):
    return lax.dot_general(a, b, (((0,), (0,)), ((), ())), precision=precision)


def mm_nt(a, b, precision=HIGH):
    return lax.dot_general(a, b, (((1,), (1,)), ((), ())), precision=precision)


class Comm:
    def a2a(self, x, axis):
        return lax.all_to_all(x, axis, 0, 0, tiled=False)

    def reduce_scatter(self, x, axis, groups):
        parts = self.a2a(x.reshape(groups, x.shape[0] // groups, *x.shape[1:]), axis)
        return jnp.sum(parts, axis=0)

    def all_gather(self, x, axis, groups):
        got = self.a2a(jnp.broadcast_to(x[None], (groups,) + x.shape), axis)
        return got.reshape(groups * x.shape[0], *x.shape[1:])

    def psum(self, x, axis, groups):
        return self.all_gather(self.reduce_scatter(x, axis, groups), axis, groups)

    def broadcast(self, x, axis, groups, root):
        parts = self.a2a(x.reshape(groups, x.shape[0] // groups, *x.shape[1:]), axis)
        return self.all_gather(parts[root], axis, groups)


def transpose_exchange(x, rows, cols):
    both = ("row", "col")
    first = []
    second = []
    for s in range(rows):
        for j in range(cols):
            src = s * cols + j
            first.append((src, (2 * j + s % 2) * cols + s // 2))
            second.append((src, (2 * j + 1 - s % 2) * cols + s // 2))
    got1 = lax.ppermute(x, both, first)
    got2 = lax.ppermute(x, both, second)
    odd_row = lax.axis_index("row") % 2 == 1
    even = jnp.where(odd_row, got2, got1)
    odd = jnp.where(odd_row, got1, got2)
    return jnp.concatenate([even, odd], axis=0)


def small_factors(gram, top):
    identity = jnp.eye(BAND, dtype=jnp.float32)
    low = jnp.linalg.cholesky(gram)
    low_inv = jax.scipy.linalg.solve_triangular(low, identity, lower=True)
    shifted = identity + mm_nt(top, low_inv)
    second = jnp.linalg.cholesky(mm_nt(shifted, shifted))
    second_inv = jax.scipy.linalg.solve_triangular(second, identity, lower=True)
    transform = mm_tn(shifted, mm_tn(second_inv, second_inv))
    return low_inv, transform


def body(a):
    comm = Comm()
    rows = lax.psum(1, "row")
    cols = lax.psum(1, "col")
    row_count, col_count = a.shape
    r = lax.axis_index("row")
    c = lax.axis_index("col")
    row_pos = r * row_count + jnp.arange(row_count, dtype=jnp.int32)
    col_pos = c * col_count + jnp.arange(col_count, dtype=jnp.int32)
    band_idx = jnp.arange(BAND, dtype=jnp.int32)
    width = PANELS * BAND

    strip = lax.psum(jnp.where(r == 0, a[:width, :], 0.0), "row")
    colb = comm.broadcast(a[:, :width], "col", cols, 0)
    lo = BAND
    p0 = jnp.where(row_pos[:, None] >= lo, colb[:, :BAND], 0.0)
    top_part = jnp.where(r == 0, colb[lo:lo + BAND, :BAND], 0.0)
    summed = comm.psum(jnp.concatenate([mm_tn(p0, p0), top_part], axis=0), "row", rows)
    gram0, top0 = summed[:BAND], summed[BAND:]
    strip_t = strip.T

    stored = []
    current = a
    prev = None
    for k in range(PANELS):
        lo = (k + 1) * BAND
        if k == 0:
            gram, top = gram0, top0
            pr = p0
            pc = jnp.where(col_pos[:, None] >= lo, strip_t[:, :BAND], 0.0)
        else:
            y_r0, w_r0, y_c0, w_c0, y_e0, w_e0 = prev
            pr = colb[:, k * BAND:(k + 1) * BAND] - mm_nt(y_r0, w_e0) - mm_nt(w_r0, y_e0)
            pc = strip_t[:, k * BAND:(k + 1) * BAND] - mm_nt(y_c0, w_e0) - mm_nt(w_c0, y_e0)
            pr = jnp.where(row_pos[:, None] >= lo, pr, 0.0)
            pc = jnp.where(col_pos[:, None] >= lo, pc, 0.0)
            top_part = jnp.where(c == 0, pc[lo:lo + BAND], 0.0)
            summed = comm.psum(jnp.concatenate([mm_tn(pc, pc), top_part], axis=0), "col", cols)
            gram, top = summed[:BAND], summed[BAND:]
        low_inv, transform = small_factors(gram, top)
        unit_r = (row_pos[:, None] - lo == band_idx[None, :]).astype(jnp.float32)
        unit_c = (col_pos[:, None] - lo == band_idx[None, :]).astype(jnp.float32)
        y_r = mm_nt(pr, low_inv) + unit_r
        y_c = mm_nt(pc, low_inv) + unit_c
        stored.append(y_r)

        xp = mm(current, y_c, FAST)
        xq = mm_tn(current, y_r, FAST)
        summed_c = comm.psum(jnp.concatenate([xq, mm_tn(y_r, xp)], axis=0), "row", rows)
        x_c = summed_c[:col_count]
        parts = [xp, summed_c[col_count:]]
        if k + 1 < PANELS:
            nlo = (k + 1) * BAND
            parts.append(mm_tn(strip_t[:, nlo:nlo + BAND], y_c))
        summed = comm.psum(jnp.concatenate(parts, axis=0), "col", cols)
        x_r = summed[:row_count]
        curv = summed[row_count:row_count + BAND]
        middle = mm_nt(mm(transform, curv), transform)
        w_r = mm_nt(x_r, transform) - 0.5 * mm(y_r, middle)
        w_c = mm_nt(x_c, transform) - 0.5 * mm(y_c, middle)
        current = current - mm_nt(y_r, w_c, FAST) - mm_nt(w_r, y_c, FAST)
        if k + 1 < PANELS:
            x_e = summed[row_count + BAND:]
            y_e = mm_nt(top, low_inv) + jnp.eye(BAND, dtype=jnp.float32)
            w_e = mm_nt(x_e, transform) - 0.5 * mm(y_e, middle)
            prev = (y_r, w_r, y_c, w_c, y_e, w_e)
    return current, jnp.concatenate(stored, axis=1)


def solution(mesh):
    return jax.shard_map(
        body,
        mesh=mesh,
        in_specs=(P("row", "col"),),
        out_specs=(P("row", "col"), P("row", None)),
        check_vma=False,
    )
```

```python
import jax
import jax.numpy as jnp
from jax import lax
from jax.sharding import PartitionSpec as P

BAND = 256
PANELS = 2
HIGH = lax.Precision.HIGHEST
FAST = lax.Precision.HIGH


def mm(a, b, precision=HIGH):
    return jnp.dot(a, b, precision=precision)


def mm_tn(a, b, precision=HIGH):
    return lax.dot_general(a, b, (((0,), (0,)), ((), ())), precision=precision)


def mm_nt(a, b, precision=HIGH):
    return lax.dot_general(a, b, (((1,), (1,)), ((), ())), precision=precision)


class Comm:
    def a2a(self, x, axis):
        return lax.all_to_all(x, axis, 0, 0, tiled=False)

    def reduce_scatter(self, x, axis, groups):
        parts = self.a2a(x.reshape(groups, x.shape[0] // groups, *x.shape[1:]), axis)
        return jnp.sum(parts, axis=0)

    def all_gather(self, x, axis, groups):
        got = self.a2a(jnp.broadcast_to(x[None], (groups,) + x.shape), axis)
        return got.reshape(groups * x.shape[0], *x.shape[1:])

    def psum(self, x, axis, groups):
        return self.all_gather(self.reduce_scatter(x, axis, groups), axis, groups)

    def broadcast(self, x, axis, groups, root):
        parts = self.a2a(x.reshape(groups, x.shape[0] // groups, *x.shape[1:]), axis)
        return self.all_gather(parts[root], axis, groups)


def transpose_exchange(x, rows, cols):
    both = ("row", "col")
    first = []
    second = []
    for s in range(rows):
        for j in range(cols):
            src = s * cols + j
            first.append((src, (2 * j + s % 2) * cols + s // 2))
            second.append((src, (2 * j + 1 - s % 2) * cols + s // 2))
    got1 = lax.ppermute(x, both, first)
    got2 = lax.ppermute(x, both, second)
    odd_row = lax.axis_index("row") % 2 == 1
    even = jnp.where(odd_row, got2, got1)
    odd = jnp.where(odd_row, got1, got2)
    return jnp.concatenate([even, odd], axis=0)


def tri_inv(low, leaf=32):
    n = low.shape[0]
    count = n // leaf
    blocks = low.reshape(count, leaf, count, leaf).transpose(0, 2, 1, 3)
    diag = blocks[jnp.arange(count), jnp.arange(count)]
    eye = jnp.broadcast_to(jnp.eye(leaf, dtype=low.dtype), diag.shape)
    inv = lax.linalg.triangular_solve(diag, eye, left_side=True, lower=True)
    size = leaf
    while size < n:
        count = n // size
        blocks = low.reshape(count, size, count, size).transpose(0, 2, 1, 3)
        even = jnp.arange(0, count, 2)
        below = blocks[even + 1, even]
        first, last = inv[0::2], inv[1::2]
        corner = -jnp.matmul(jnp.matmul(last, below, precision=HIGH), first, precision=HIGH)
        zeros = jnp.zeros_like(first)
        top_half = jnp.concatenate([first, zeros], axis=2)
        bottom_half = jnp.concatenate([corner, last], axis=2)
        inv = jnp.concatenate([top_half, bottom_half], axis=1)
        size *= 2
    return inv[0]


def small_factors(gram, top):
    identity = jnp.eye(BAND, dtype=jnp.float32)
    low_inv = tri_inv(jnp.linalg.cholesky(gram))
    shifted = identity + mm_nt(top, low_inv)
    second_inv = tri_inv(jnp.linalg.cholesky(mm_nt(shifted, shifted)))
    transform = mm_tn(shifted, mm_tn(second_inv, second_inv))
    return low_inv, transform


def body(a):
    comm = Comm()
    rows = lax.psum(1, "row")
    cols = lax.psum(1, "col")
    row_count, col_count = a.shape
    r = lax.axis_index("row")
    c = lax.axis_index("col")
    row_pos = r * row_count + jnp.arange(row_count, dtype=jnp.int32)
    col_pos = c * col_count + jnp.arange(col_count, dtype=jnp.int32)
    band_idx = jnp.arange(BAND, dtype=jnp.int32)
    width = PANELS * BAND

    strip = lax.psum(jnp.where(r == 0, a[:width, :], 0.0), "row")
    colb = comm.broadcast(a[:, :width], "col", cols, 0)
    lo = BAND
    p0 = jnp.where(row_pos[:, None] >= lo, colb[:, :BAND], 0.0)
    top_part = jnp.where(r == 0, colb[lo:lo + BAND, :BAND], 0.0)
    summed = comm.psum(jnp.concatenate([mm_tn(p0, p0), top_part], axis=0), "row", rows)
    gram0, top0 = summed[:BAND], summed[BAND:]
    strip_t = strip.T

    stored = []
    current = a
    prev = None
    for k in range(PANELS):
        lo = (k + 1) * BAND
        if k == 0:
            gram, top = gram0, top0
            pr = p0
            pc = jnp.where(col_pos[:, None] >= lo, strip_t[:, :BAND], 0.0)
        else:
            y_r0, w_r0, y_c0, w_c0, y_e0, w_e0 = prev
            pr = colb[:, k * BAND:(k + 1) * BAND] - mm_nt(y_r0, w_e0) - mm_nt(w_r0, y_e0)
            pc = strip_t[:, k * BAND:(k + 1) * BAND] - mm_nt(y_c0, w_e0) - mm_nt(w_c0, y_e0)
            pr = jnp.where(row_pos[:, None] >= lo, pr, 0.0)
            pc = jnp.where(col_pos[:, None] >= lo, pc, 0.0)
            top_part = jnp.where(c == 0, pc[lo:lo + BAND], 0.0)
            summed = comm.psum(jnp.concatenate([mm_tn(pc, pc), top_part], axis=0), "col", cols)
            gram, top = summed[:BAND], summed[BAND:]
        low_inv, transform = small_factors(gram, top)
        unit_r = (row_pos[:, None] - lo == band_idx[None, :]).astype(jnp.float32)
        unit_c = (col_pos[:, None] - lo == band_idx[None, :]).astype(jnp.float32)
        y_r = mm_nt(pr, low_inv) + unit_r
        y_c = mm_nt(pc, low_inv) + unit_c
        stored.append(y_r)

        xp = mm(current, y_c, FAST)
        xq = mm_tn(current, y_r, FAST)
        summed_c = comm.psum(jnp.concatenate([xq, mm_tn(y_r, xp)], axis=0), "row", rows)
        x_c = summed_c[:col_count]
        parts = [xp, summed_c[col_count:]]
        if k + 1 < PANELS:
            nlo = (k + 1) * BAND
            parts.append(mm_tn(strip_t[:, nlo:nlo + BAND], y_c))
        summed = comm.psum(jnp.concatenate(parts, axis=0), "col", cols)
        x_r = summed[:row_count]
        curv = summed[row_count:row_count + BAND]
        middle = mm_nt(mm(transform, curv), transform)
        w_r = mm_nt(x_r, transform) - 0.5 * mm(y_r, middle)
        w_c = mm_nt(x_c, transform) - 0.5 * mm(y_c, middle)
        current = current - mm_nt(y_r, w_c, FAST) - mm_nt(w_r, y_c, FAST)
        if k + 1 < PANELS:
            x_e = summed[row_count + BAND:]
            y_e = mm_nt(top, low_inv) + jnp.eye(BAND, dtype=jnp.float32)
            w_e = mm_nt(x_e, transform) - 0.5 * mm(y_e, middle)
            prev = (y_r, w_r, y_c, w_c, y_e, w_e)
    return current, jnp.concatenate(stored, axis=1)


def solution(mesh):
    return jax.shard_map(
        body,
        mesh=mesh,
        in_specs=(P("row", "col"),),
        out_specs=(P("row", "col"), P("row", None)),
        check_vma=False,
    )
```

```python
import jax
import jax.numpy as jnp
from jax import lax
from jax.sharding import PartitionSpec as P

BAND = 256
PANELS = 2
HIGH = lax.Precision.HIGHEST
FAST = lax.Precision.HIGH


def mm(a, b, precision=HIGH):
    return jnp.dot(a, b, precision=precision)


def mm_tn(a, b, precision=HIGH):
    return lax.dot_general(a, b, (((0,), (0,)), ((), ())), precision=precision)


def mm_nt(a, b, precision=HIGH):
    return lax.dot_general(a, b, (((1,), (1,)), ((), ())), precision=precision)


class Comm:
    def a2a(self, x, axis):
        return lax.all_to_all(x, axis, 0, 0, tiled=False)

    def reduce_scatter(self, x, axis, groups):
        parts = self.a2a(x.reshape(groups, x.shape[0] // groups, *x.shape[1:]), axis)
        return jnp.sum(parts, axis=0)

    def all_gather(self, x, axis, groups):
        got = self.a2a(jnp.broadcast_to(x[None], (groups,) + x.shape), axis)
        return got.reshape(groups * x.shape[0], *x.shape[1:])

    def psum(self, x, axis, groups):
        return self.all_gather(self.reduce_scatter(x, axis, groups), axis, groups)

    def broadcast(self, x, axis, groups, root):
        parts = self.a2a(x.reshape(groups, x.shape[0] // groups, *x.shape[1:]), axis)
        return self.all_gather(parts[root], axis, groups)


def transpose_exchange(x, rows, cols):
    both = ("row", "col")
    first = []
    second = []
    for s in range(rows):
        for j in range(cols):
            src = s * cols + j
            first.append((src, (2 * j + s % 2) * cols + s // 2))
            second.append((src, (2 * j + 1 - s % 2) * cols + s // 2))
    got1 = lax.ppermute(x, both, first)
    got2 = lax.ppermute(x, both, second)
    odd_row = lax.axis_index("row") % 2 == 1
    even = jnp.where(odd_row, got2, got1)
    odd = jnp.where(odd_row, got1, got2)
    return jnp.concatenate([even, odd], axis=0)


def small_factors(gram, top):
    identity = jnp.eye(BAND, dtype=jnp.float32)
    low = jnp.linalg.cholesky(gram)
    low_inv = jax.scipy.linalg.solve_triangular(low, identity, lower=True)
    shifted = identity + mm_nt(top, low_inv)
    second = jnp.linalg.cholesky(mm_nt(shifted, shifted))
    second_inv = jax.scipy.linalg.solve_triangular(second, identity, lower=True)
    transform = mm_tn(shifted, mm_tn(second_inv, second_inv))
    return low_inv, transform


def body(a):
    comm = Comm()
    rows = lax.psum(1, "row")
    cols = lax.psum(1, "col")
    row_count, col_count = a.shape
    r = lax.axis_index("row")
    c = lax.axis_index("col")
    row_pos = r * row_count + jnp.arange(row_count, dtype=jnp.int32)
    col_pos = c * col_count + jnp.arange(col_count, dtype=jnp.int32)
    band_idx = jnp.arange(BAND, dtype=jnp.int32)
    width = PANELS * BAND

    strip = lax.psum(jnp.where(r == 0, a[:width, :], 0.0), "row")
    lo = BAND
    p0_own = jnp.where(row_pos[:, None] >= lo, a[:, :BAND], 0.0)
    own = jnp.concatenate([mm_tn(p0_own, p0_own), jnp.where(r == 0, a[lo:lo + BAND, :BAND], 0.0)], axis=0)
    own = jnp.where(c == 0, own, 0.0)
    summed = comm.psum(own.reshape(rows * cols, -1, 128), ("row", "col"), rows * cols)
    summed = summed.reshape(2 * BAND, BAND)
    gram0, top0 = summed[:BAND], summed[BAND:]
    colb = comm.broadcast(a[:, :width], "col", cols, 0)
    p0 = jnp.where(row_pos[:, None] >= lo, colb[:, :BAND], 0.0)
    strip_t = strip.T

    stored = []
    current = a
    prev = None
    for k in range(PANELS):
        lo = (k + 1) * BAND
        if k == 0:
            gram, top = gram0, top0
            pr = p0
            pc = jnp.where(col_pos[:, None] >= lo, strip_t[:, :BAND], 0.0)
        else:
            y_r0, w_r0, y_c0, w_c0, y_e0, w_e0 = prev
            pr = colb[:, k * BAND:(k + 1) * BAND] - mm_nt(y_r0, w_e0) - mm_nt(w_r0, y_e0)
            pc = strip_t[:, k * BAND:(k + 1) * BAND] - mm_nt(y_c0, w_e0) - mm_nt(w_c0, y_e0)
            pr = jnp.where(row_pos[:, None] >= lo, pr, 0.0)
            pc = jnp.where(col_pos[:, None] >= lo, pc, 0.0)
            top_part = jnp.where(c == 0, pc[lo:lo + BAND], 0.0)
            summed = comm.psum(jnp.concatenate([mm_tn(pc, pc), top_part], axis=0), "col", cols)
            gram, top = summed[:BAND], summed[BAND:]
        low_inv, transform = small_factors(gram, top)
        unit_r = (row_pos[:, None] - lo == band_idx[None, :]).astype(jnp.float32)
        unit_c = (col_pos[:, None] - lo == band_idx[None, :]).astype(jnp.float32)
        y_r = mm_nt(pr, low_inv) + unit_r
        y_c = mm_nt(pc, low_inv) + unit_c
        stored.append(y_r)

        xp = mm(current, y_c, FAST)
        xq = mm_tn(current, y_r, FAST)
        summed_c = comm.psum(jnp.concatenate([xq, mm_tn(y_r, xp)], axis=0), "row", rows)
        x_c = summed_c[:col_count]
        parts = [xp, summed_c[col_count:]]
        if k + 1 < PANELS:
            nlo = (k + 1) * BAND
            parts.append(mm_tn(strip_t[:, nlo:nlo + BAND], y_c))
        summed = comm.psum(jnp.concatenate(parts, axis=0), "col", cols)
        x_r = summed[:row_count]
        curv = summed[row_count:row_count + BAND]
        middle = mm_nt(mm(transform, curv), transform)
        w_r = mm_nt(x_r, transform) - 0.5 * mm(y_r, middle)
        w_c = mm_nt(x_c, transform) - 0.5 * mm(y_c, middle)
        current = current - mm_nt(y_r, w_c, FAST) - mm_nt(w_r, y_c, FAST)
        if k + 1 < PANELS:
            x_e = summed[row_count + BAND:]
            y_e = mm_nt(top, low_inv) + jnp.eye(BAND, dtype=jnp.float32)
            w_e = mm_nt(x_e, transform) - 0.5 * mm(y_e, middle)
            prev = (y_r, w_r, y_c, w_c, y_e, w_e)
    return current, jnp.concatenate(stored, axis=1)


def solution(mesh):
    return jax.shard_map(
        body,
        mesh=mesh,
        in_specs=(P("row", "col"),),
        out_specs=(P("row", "col"), P("row", None)),
        check_vma=False,
    )
```

```python
import jax
import jax.numpy as jnp
from jax import lax
from jax.sharding import PartitionSpec as P

BAND = 256
PANELS = 2
HIGH = lax.Precision.HIGHEST
FAST = lax.Precision.HIGH


def mm(a, b, precision=HIGH):
    return jnp.dot(a, b, precision=precision)


def mm_tn(a, b, precision=HIGH):
    return lax.dot_general(a, b, (((0,), (0,)), ((), ())), precision=precision)


def mm_nt(a, b, precision=HIGH):
    return lax.dot_general(a, b, (((1,), (1,)), ((), ())), precision=precision)


class Comm:
    def a2a(self, x, axis):
        return lax.all_to_all(x, axis, 0, 0, tiled=False)

    def reduce_scatter(self, x, axis, groups):
        parts = self.a2a(x.reshape(groups, x.shape[0] // groups, *x.shape[1:]), axis)
        return jnp.sum(parts, axis=0)

    def all_gather(self, x, axis, groups):
        got = self.a2a(jnp.broadcast_to(x[None], (groups,) + x.shape), axis)
        return got.reshape(groups * x.shape[0], *x.shape[1:])

    def psum(self, x, axis, groups):
        return self.all_gather(self.reduce_scatter(x, axis, groups), axis, groups)

    def broadcast(self, x, axis, groups, root):
        parts = self.a2a(x.reshape(groups, x.shape[0] // groups, *x.shape[1:]), axis)
        return self.all_gather(parts[root], axis, groups)


def transpose_exchange(x, rows, cols):
    both = ("row", "col")
    first = []
    second = []
    for s in range(rows):
        for j in range(cols):
            src = s * cols + j
            first.append((src, (2 * j + s % 2) * cols + s // 2))
            second.append((src, (2 * j + 1 - s % 2) * cols + s // 2))
    got1 = lax.ppermute(x, both, first)
    got2 = lax.ppermute(x, both, second)
    odd_row = lax.axis_index("row") % 2 == 1
    even = jnp.where(odd_row, got2, got1)
    odd = jnp.where(odd_row, got1, got2)
    return jnp.concatenate([even, odd], axis=0)


def small_factors(gram, top):
    identity = jnp.eye(BAND, dtype=jnp.float32)
    low = jnp.linalg.cholesky(gram)
    low_inv = jax.scipy.linalg.solve_triangular(low, identity, lower=True)
    shifted = identity + mm_nt(top, low_inv)
    second = jnp.linalg.cholesky(mm_nt(shifted, shifted))
    second_inv = jax.scipy.linalg.solve_triangular(second, identity, lower=True)
    transform = mm_tn(shifted, mm_tn(second_inv, second_inv))
    return low_inv, transform


def body(a):
    comm = Comm()
    rows = lax.psum(1, "row")
    cols = lax.psum(1, "col")
    row_count, col_count = a.shape
    r = lax.axis_index("row")
    c = lax.axis_index("col")
    row_pos = r * row_count + jnp.arange(row_count, dtype=jnp.int32)
    col_pos = c * col_count + jnp.arange(col_count, dtype=jnp.int32)
    band_idx = jnp.arange(BAND, dtype=jnp.int32)
    width = PANELS * BAND

    strip_parts = []
    for k in range(PANELS):
        rows_k = jnp.where(r == 0, a[k * BAND:(k + 1) * BAND, :], 0.0)
        if strip_parts:
            rows_k, _ = lax.optimization_barrier((rows_k, strip_parts[-1]))
        strip_parts.append(lax.psum(rows_k, "row"))
    lo = BAND
    p0_own = jnp.where(row_pos[:, None] >= lo, a[:, :BAND], 0.0)
    own = jnp.concatenate([mm_tn(p0_own, p0_own), jnp.where(r == 0, a[lo:lo + BAND, :BAND], 0.0)], axis=0)
    own = jnp.where(c == 0, own, 0.0)
    summed = comm.psum(own.reshape(rows * cols, -1, 128), ("row", "col"), rows * cols)
    summed = summed.reshape(2 * BAND, BAND)
    gram0, top0 = summed[:BAND], summed[BAND:]
    colb = comm.broadcast(a[:, :width], "col", cols, 0)
    p0 = jnp.where(row_pos[:, None] >= lo, colb[:, :BAND], 0.0)
    strip_t = [part.T for part in strip_parts]

    stored = []
    current = a
    prev = None
    for k in range(PANELS):
        lo = (k + 1) * BAND
        if k == 0:
            gram, top = gram0, top0
            pr = p0
            pc = jnp.where(col_pos[:, None] >= lo, strip_t[0], 0.0)
        else:
            y_r0, w_r0, y_c0, w_c0, y_e0, w_e0 = prev
            pr = colb[:, k * BAND:(k + 1) * BAND] - mm_nt(y_r0, w_e0) - mm_nt(w_r0, y_e0)
            pc = strip_t[k] - mm_nt(y_c0, w_e0) - mm_nt(w_c0, y_e0)
            pr = jnp.where(row_pos[:, None] >= lo, pr, 0.0)
            pc = jnp.where(col_pos[:, None] >= lo, pc, 0.0)
            top_part = jnp.where(c == 0, pc[lo:lo + BAND], 0.0)
            summed = comm.psum(jnp.concatenate([mm_tn(pc, pc), top_part], axis=0), "col", cols)
            gram, top = summed[:BAND], summed[BAND:]
        low_inv, transform = small_factors(gram, top)
        unit_r = (row_pos[:, None] - lo == band_idx[None, :]).astype(jnp.float32)
        unit_c = (col_pos[:, None] - lo == band_idx[None, :]).astype(jnp.float32)
        y_r = mm_nt(pr, low_inv) + unit_r
        y_c = mm_nt(pc, low_inv) + unit_c
        stored.append(y_r)

        xp = mm(current, y_c, FAST)
        xq = mm_tn(current, y_r, FAST)
        summed_c = comm.psum(jnp.concatenate([xq, mm_tn(y_r, xp)], axis=0), "row", rows)
        x_c = summed_c[:col_count]
        parts = [xp, summed_c[col_count:]]
        if k + 1 < PANELS:
            nlo = (k + 1) * BAND
            parts.append(mm_tn(strip_t[k + 1], y_c))
        summed = comm.psum(jnp.concatenate(parts, axis=0), "col", cols)
        x_r = summed[:row_count]
        curv = summed[row_count:row_count + BAND]
        middle = mm_nt(mm(transform, curv), transform)
        w_r = mm_nt(x_r, transform) - 0.5 * mm(y_r, middle)
        w_c = mm_nt(x_c, transform) - 0.5 * mm(y_c, middle)
        current = current - mm_nt(y_r, w_c, FAST) - mm_nt(w_r, y_c, FAST)
        if k + 1 < PANELS:
            x_e = summed[row_count + BAND:]
            y_e = mm_nt(top, low_inv) + jnp.eye(BAND, dtype=jnp.float32)
            w_e = mm_nt(x_e, transform) - 0.5 * mm(y_e, middle)
            prev = (y_r, w_r, y_c, w_c, y_e, w_e)
    return current, jnp.concatenate(stored, axis=1)


def solution(mesh):
    return jax.shard_map(
        body,
        mesh=mesh,
        in_specs=(P("row", "col"),),
        out_specs=(P("row", "col"), P("row", None)),
        check_vma=False,
    )
```

```python
import jax
import jax.numpy as jnp
from jax import lax
from jax.sharding import PartitionSpec as P

BAND = 256
PANELS = 2
HIGH = lax.Precision.HIGHEST
FAST = lax.Precision.HIGH


def mm(a, b, precision=HIGH):
    return jnp.dot(a, b, precision=precision)


def mm_tn(a, b, precision=HIGH):
    return lax.dot_general(a, b, (((0,), (0,)), ((), ())), precision=precision)


def mm_nt(a, b, precision=HIGH):
    return lax.dot_general(a, b, (((1,), (1,)), ((), ())), precision=precision)


class Comm:
    def a2a(self, x, axis):
        return lax.all_to_all(x, axis, 0, 0, tiled=False)

    def reduce_scatter(self, x, axis, groups):
        parts = self.a2a(x.reshape(groups, x.shape[0] // groups, *x.shape[1:]), axis)
        return jnp.sum(parts, axis=0)

    def all_gather(self, x, axis, groups):
        got = self.a2a(jnp.broadcast_to(x[None], (groups,) + x.shape), axis)
        return got.reshape(groups * x.shape[0], *x.shape[1:])

    def psum(self, x, axis, groups):
        return self.all_gather(self.reduce_scatter(x, axis, groups), axis, groups)

    def broadcast(self, x, axis, groups, root):
        parts = self.a2a(x.reshape(groups, x.shape[0] // groups, *x.shape[1:]), axis)
        return self.all_gather(parts[root], axis, groups)


def transpose_exchange(x, rows, cols):
    both = ("row", "col")
    first = []
    second = []
    for s in range(rows):
        for j in range(cols):
            src = s * cols + j
            first.append((src, (2 * j + s % 2) * cols + s // 2))
            second.append((src, (2 * j + 1 - s % 2) * cols + s // 2))
    got1 = lax.ppermute(x, both, first)
    got2 = lax.ppermute(x, both, second)
    odd_row = lax.axis_index("row") % 2 == 1
    even = jnp.where(odd_row, got2, got1)
    odd = jnp.where(odd_row, got1, got2)
    return jnp.concatenate([even, odd], axis=0)


def cholesky_inverse(spd):
    half = spd.shape[0] // 2
    identity = jnp.eye(half, dtype=spd.dtype)
    low11 = jnp.linalg.cholesky(spd[:half, :half])
    inv11 = jax.scipy.linalg.solve_triangular(low11, identity, lower=True)
    low21 = mm_nt(spd[half:, :half], inv11)
    low22 = jnp.linalg.cholesky(spd[half:, half:] - mm_nt(low21, low21))
    inv22 = jax.scipy.linalg.solve_triangular(low22, identity, lower=True)
    inv21 = -mm(mm(inv22, low21), inv11)
    upper = jnp.concatenate([inv11, jnp.zeros_like(inv11)], axis=1)
    lower = jnp.concatenate([inv21, inv22], axis=1)
    return jnp.concatenate([upper, lower], axis=0)


def small_factors(gram, top):
    identity = jnp.eye(BAND, dtype=jnp.float32)
    low_inv = cholesky_inverse(gram)
    shifted = identity + mm_nt(top, low_inv)
    second_inv = cholesky_inverse(mm_nt(shifted, shifted))
    transform = mm_tn(shifted, mm_tn(second_inv, second_inv))
    return low_inv, transform


def body(a):
    comm = Comm()
    rows = lax.psum(1, "row")
    cols = lax.psum(1, "col")
    row_count, col_count = a.shape
    r = lax.axis_index("row")
    c = lax.axis_index("col")
    row_pos = r * row_count + jnp.arange(row_count, dtype=jnp.int32)
    col_pos = c * col_count + jnp.arange(col_count, dtype=jnp.int32)
    band_idx = jnp.arange(BAND, dtype=jnp.int32)
    width = PANELS * BAND

    strip = lax.psum(jnp.where(r == 0, a[:width, :], 0.0), "row")
    lo = BAND
    p0_own = jnp.where(row_pos[:, None] >= lo, a[:, :BAND], 0.0)
    own = jnp.concatenate([mm_tn(p0_own, p0_own), jnp.where(r == 0, a[lo:lo + BAND, :BAND], 0.0)], axis=0)
    own = jnp.where(c == 0, own, 0.0)
    summed = comm.psum(own.reshape(rows * cols, -1, 128), ("row", "col"), rows * cols)
    summed = summed.reshape(2 * BAND, BAND)
    gram0, top0 = summed[:BAND], summed[BAND:]
    colb = comm.broadcast(a[:, :width], "col", cols, 0)
    p0 = jnp.where(row_pos[:, None] >= lo, colb[:, :BAND], 0.0)
    strip_t = strip.T

    stored = []
    current = a
    prev = None
    for k in range(PANELS):
        lo = (k + 1) * BAND
        if k == 0:
            gram, top = gram0, top0
            pr = p0
            pc = jnp.where(col_pos[:, None] >= lo, strip_t[:, :BAND], 0.0)
        else:
            y_r0, w_r0, y_c0, w_c0, y_e0, w_e0 = prev
            pr = colb[:, k * BAND:(k + 1) * BAND] - mm_nt(y_r0, w_e0) - mm_nt(w_r0, y_e0)
            pc = strip_t[:, k * BAND:(k + 1) * BAND] - mm_nt(y_c0, w_e0) - mm_nt(w_c0, y_e0)
            pr = jnp.where(row_pos[:, None] >= lo, pr, 0.0)
            pc = jnp.where(col_pos[:, None] >= lo, pc, 0.0)
            top_part = jnp.where(c == 0, pc[lo:lo + BAND], 0.0)
            summed = comm.psum(jnp.concatenate([mm_tn(pc, pc), top_part], axis=0), "col", cols)
            gram, top = summed[:BAND], summed[BAND:]
        low_inv, transform = small_factors(gram, top)
        unit_r = (row_pos[:, None] - lo == band_idx[None, :]).astype(jnp.float32)
        unit_c = (col_pos[:, None] - lo == band_idx[None, :]).astype(jnp.float32)
        y_r = mm_nt(pr, low_inv) + unit_r
        y_c = mm_nt(pc, low_inv) + unit_c
        stored.append(y_r)

        xp = mm(current, y_c, FAST)
        xq = mm_tn(current, y_r, FAST)
        summed_c = comm.psum(jnp.concatenate([xq, mm_tn(y_r, xp)], axis=0), "row", rows)
        x_c = summed_c[:col_count]
        parts = [xp, summed_c[col_count:]]
        if k + 1 < PANELS:
            nlo = (k + 1) * BAND
            parts.append(mm_tn(strip_t[:, nlo:nlo + BAND], y_c))
        summed = comm.psum(jnp.concatenate(parts, axis=0), "col", cols)
        x_r = summed[:row_count]
        curv = summed[row_count:row_count + BAND]
        middle = mm_nt(mm(transform, curv), transform)
        w_r = mm_nt(x_r, transform) - 0.5 * mm(y_r, middle)
        w_c = mm_nt(x_c, transform) - 0.5 * mm(y_c, middle)
        current = current - mm_nt(y_r, w_c, FAST) - mm_nt(w_r, y_c, FAST)
        if k + 1 < PANELS:
            x_e = summed[row_count + BAND:]
            y_e = mm_nt(top, low_inv) + jnp.eye(BAND, dtype=jnp.float32)
            w_e = mm_nt(x_e, transform) - 0.5 * mm(y_e, middle)
            prev = (y_r, w_r, y_c, w_c, y_e, w_e)
    return current, jnp.concatenate(stored, axis=1)


def solution(mesh):
    return jax.shard_map(
        body,
        mesh=mesh,
        in_specs=(P("row", "col"),),
        out_specs=(P("row", "col"), P("row", None)),
        check_vma=False,
    )
```

```python
import jax
import jax.numpy as jnp
from jax import lax
from jax.sharding import PartitionSpec as P

BAND = 256
PANELS = 2
HIGH = lax.Precision.HIGHEST
FAST = lax.Precision.HIGH


def mm(a, b, precision=HIGH):
    return jnp.dot(a, b, precision=precision)


def mm_tn(a, b, precision=HIGH):
    return lax.dot_general(a, b, (((0,), (0,)), ((), ())), precision=precision)


def mm_nt(a, b, precision=HIGH):
    return lax.dot_general(a, b, (((1,), (1,)), ((), ())), precision=precision)


class Comm:
    def a2a(self, x, axis):
        return lax.all_to_all(x, axis, 0, 0, tiled=False)

    def reduce_scatter(self, x, axis, groups):
        parts = self.a2a(x.reshape(groups, x.shape[0] // groups, *x.shape[1:]), axis)
        return jnp.sum(parts, axis=0)

    def all_gather(self, x, axis, groups):
        got = self.a2a(jnp.broadcast_to(x[None], (groups,) + x.shape), axis)
        return got.reshape(groups * x.shape[0], *x.shape[1:])

    def psum(self, x, axis, groups):
        return self.all_gather(self.reduce_scatter(x, axis, groups), axis, groups)

    def broadcast(self, x, axis, groups, root):
        parts = self.a2a(x.reshape(groups, x.shape[0] // groups, *x.shape[1:]), axis)
        return self.all_gather(parts[root], axis, groups)


def transpose_exchange(x, rows, cols):
    both = ("row", "col")
    first = []
    second = []
    for s in range(rows):
        for j in range(cols):
            src = s * cols + j
            first.append((src, (2 * j + s % 2) * cols + s // 2))
            second.append((src, (2 * j + 1 - s % 2) * cols + s // 2))
    got1 = lax.ppermute(x, both, first)
    got2 = lax.ppermute(x, both, second)
    odd_row = lax.axis_index("row") % 2 == 1
    even = jnp.where(odd_row, got2, got1)
    odd = jnp.where(odd_row, got1, got2)
    return jnp.concatenate([even, odd], axis=0)


def cholesky_inverse(spd):
    half = spd.shape[0] // 2
    identity = jnp.eye(half, dtype=spd.dtype)
    low11 = jnp.linalg.cholesky(spd[:half, :half])
    inv11 = jax.scipy.linalg.solve_triangular(low11, identity, lower=True)
    low21 = mm_nt(spd[half:, :half], inv11)
    low22 = jnp.linalg.cholesky(spd[half:, half:] - mm_nt(low21, low21))
    inv22 = jax.scipy.linalg.solve_triangular(low22, identity, lower=True)
    inv21 = -mm(mm(inv22, low21), inv11)
    upper = jnp.concatenate([inv11, jnp.zeros_like(inv11)], axis=1)
    lower = jnp.concatenate([inv21, inv22], axis=1)
    return jnp.concatenate([upper, lower], axis=0)


def small_factors(gram, top):
    identity = jnp.eye(BAND, dtype=jnp.float32)
    low_inv = cholesky_inverse(gram)
    shifted = identity + mm_nt(top, low_inv)
    second_inv = cholesky_inverse(mm_nt(shifted, shifted))
    transform = mm_tn(shifted, mm_tn(second_inv, second_inv))
    return low_inv, transform


def body(a):
    comm = Comm()
    rows = lax.psum(1, "row")
    cols = lax.psum(1, "col")
    row_count, col_count = a.shape
    r = lax.axis_index("row")
    c = lax.axis_index("col")
    row_pos = r * row_count + jnp.arange(row_count, dtype=jnp.int32)
    col_pos = c * col_count + jnp.arange(col_count, dtype=jnp.int32)
    band_idx = jnp.arange(BAND, dtype=jnp.int32)
    width = PANELS * BAND

    strip_parts = []
    for k in range(PANELS):
        rows_k = jnp.where(r == 0, a[k * BAND:(k + 1) * BAND, :], 0.0)
        if strip_parts:
            rows_k, _ = lax.optimization_barrier((rows_k, strip_parts[-1]))
        strip_parts.append(lax.psum(rows_k, "row"))
    lo = BAND
    p0_own = jnp.where(row_pos[:, None] >= lo, a[:, :BAND], 0.0)
    own = jnp.concatenate([mm_tn(p0_own, p0_own), jnp.where(r == 0, a[lo:lo + BAND, :BAND], 0.0)], axis=0)
    own = jnp.where(c == 0, own, 0.0)
    summed = comm.psum(own.reshape(rows * cols, -1, 128), ("row", "col"), rows * cols)
    summed = summed.reshape(2 * BAND, BAND)
    gram0, top0 = summed[:BAND], summed[BAND:]
    colb = comm.broadcast(a[:, :width], "col", cols, 0)
    p0 = jnp.where(row_pos[:, None] >= lo, colb[:, :BAND], 0.0)
    strip_t = [part.T for part in strip_parts]

    stored = []
    current = a
    prev = None
    for k in range(PANELS):
        lo = (k + 1) * BAND
        if k == 0:
            gram, top = gram0, top0
            pr = p0
            pc = jnp.where(col_pos[:, None] >= lo, strip_t[0], 0.0)
        else:
            y_r0, w_r0, y_c0, w_c0, y_e0, w_e0 = prev
            pr = colb[:, k * BAND:(k + 1) * BAND] - mm_nt(y_r0, w_e0) - mm_nt(w_r0, y_e0)
            pc = strip_t[k] - mm_nt(y_c0, w_e0) - mm_nt(w_c0, y_e0)
            pr = jnp.where(row_pos[:, None] >= lo, pr, 0.0)
            pc = jnp.where(col_pos[:, None] >= lo, pc, 0.0)
            top_part = jnp.where(c == 0, pc[lo:lo + BAND], 0.0)
            summed = comm.psum(jnp.concatenate([mm_tn(pc, pc), top_part], axis=0), "col", cols)
            gram, top = summed[:BAND], summed[BAND:]
        low_inv, transform = small_factors(gram, top)
        unit_r = (row_pos[:, None] - lo == band_idx[None, :]).astype(jnp.float32)
        unit_c = (col_pos[:, None] - lo == band_idx[None, :]).astype(jnp.float32)
        y_r = mm_nt(pr, low_inv) + unit_r
        y_c = mm_nt(pc, low_inv) + unit_c
        stored.append(y_r)

        xp = mm(current, y_c, FAST)
        xq = mm_tn(current, y_r, FAST)
        row_parts = [xq, mm_tn(y_r, xp)]
        if k + 1 < PANELS:
            nlo = (k + 1) * BAND
            row_parts.append(mm_tn(colb[:, nlo:nlo + BAND], y_r))
        summed_c = comm.psum(jnp.concatenate(row_parts, axis=0), "row", rows)
        x_c = summed_c[:col_count]
        summed = comm.psum(jnp.concatenate([xp, summed_c[col_count:col_count + BAND]], axis=0), "col", cols)
        x_r = summed[:row_count]
        curv = summed[row_count:row_count + BAND]
        middle = mm_nt(mm(transform, curv), transform)
        w_r = mm_nt(x_r, transform) - 0.5 * mm(y_r, middle)
        w_c = mm_nt(x_c, transform) - 0.5 * mm(y_c, middle)
        current = current - mm_nt(y_r, w_c, FAST) - mm_nt(w_r, y_c, FAST)
        if k + 1 < PANELS:
            x_e = summed_c[col_count + BAND:]
            y_e = mm_nt(top, low_inv) + jnp.eye(BAND, dtype=jnp.float32)
            w_e = mm_nt(x_e, transform) - 0.5 * mm(y_e, middle)
            prev = (y_r, w_r, y_c, w_c, y_e, w_e)
    return current, jnp.concatenate(stored, axis=1)


def solution(mesh):
    return jax.shard_map(
        body,
        mesh=mesh,
        in_specs=(P("row", "col"),),
        out_specs=(P("row", "col"), P("row", None)),
        check_vma=False,
    )
```

```python
import jax
import jax.numpy as jnp
from jax import lax
from jax.sharding import PartitionSpec as P

BAND = 256
PANELS = 2
HIGH = lax.Precision.HIGH
FAST = lax.Precision.HIGH


def mm(a, b, precision=HIGH):
    return jnp.dot(a, b, precision=precision)


def mm_tn(a, b, precision=HIGH):
    return lax.dot_general(a, b, (((0,), (0,)), ((), ())), precision=precision)


def mm_nt(a, b, precision=HIGH):
    return lax.dot_general(a, b, (((1,), (1,)), ((), ())), precision=precision)


class Comm:
    def a2a(self, x, axis):
        return lax.all_to_all(x, axis, 0, 0, tiled=False)

    def reduce_scatter(self, x, axis, groups):
        parts = self.a2a(x.reshape(groups, x.shape[0] // groups, *x.shape[1:]), axis)
        return jnp.sum(parts, axis=0)

    def all_gather(self, x, axis, groups):
        got = self.a2a(jnp.broadcast_to(x[None], (groups,) + x.shape), axis)
        return got.reshape(groups * x.shape[0], *x.shape[1:])

    def psum(self, x, axis, groups):
        return self.all_gather(self.reduce_scatter(x, axis, groups), axis, groups)

    def broadcast(self, x, axis, groups, root):
        parts = self.a2a(x.reshape(groups, x.shape[0] // groups, *x.shape[1:]), axis)
        return self.all_gather(parts[root], axis, groups)


def transpose_exchange(x, rows, cols):
    both = ("row", "col")
    first = []
    second = []
    for s in range(rows):
        for j in range(cols):
            src = s * cols + j
            first.append((src, (2 * j + s % 2) * cols + s // 2))
            second.append((src, (2 * j + 1 - s % 2) * cols + s // 2))
    got1 = lax.ppermute(x, both, first)
    got2 = lax.ppermute(x, both, second)
    odd_row = lax.axis_index("row") % 2 == 1
    even = jnp.where(odd_row, got2, got1)
    odd = jnp.where(odd_row, got1, got2)
    return jnp.concatenate([even, odd], axis=0)


def cholesky_inverse(spd):
    half = spd.shape[0] // 2
    identity = jnp.eye(half, dtype=spd.dtype)
    low11 = jnp.linalg.cholesky(spd[:half, :half])
    inv11 = jax.scipy.linalg.solve_triangular(low11, identity, lower=True)
    low21 = mm_nt(spd[half:, :half], inv11)
    low22 = jnp.linalg.cholesky(spd[half:, half:] - mm_nt(low21, low21))
    inv22 = jax.scipy.linalg.solve_triangular(low22, identity, lower=True)
    inv21 = -mm(mm(inv22, low21), inv11)
    upper = jnp.concatenate([inv11, jnp.zeros_like(inv11)], axis=1)
    lower = jnp.concatenate([inv21, inv22], axis=1)
    return jnp.concatenate([upper, lower], axis=0)


def small_factors(gram, top):
    identity = jnp.eye(BAND, dtype=jnp.float32)
    low_inv = cholesky_inverse(gram)
    shifted = identity + mm_nt(top, low_inv)
    second_inv = cholesky_inverse(mm_nt(shifted, shifted))
    transform = mm_tn(shifted, mm_tn(second_inv, second_inv))
    return low_inv, transform


def body(a):
    comm = Comm()
    rows = lax.psum(1, "row")
    cols = lax.psum(1, "col")
    row_count, col_count = a.shape
    r = lax.axis_index("row")
    c = lax.axis_index("col")
    row_pos = r * row_count + jnp.arange(row_count, dtype=jnp.int32)
    col_pos = c * col_count + jnp.arange(col_count, dtype=jnp.int32)
    band_idx = jnp.arange(BAND, dtype=jnp.int32)
    width = PANELS * BAND

    strip = lax.psum(jnp.where(r == 0, a[:width, :], 0.0), "row")
    lo = BAND
    p0_own = jnp.where(row_pos[:, None] >= lo, a[:, :BAND], 0.0)
    own = jnp.concatenate([mm_tn(p0_own, p0_own), jnp.where(r == 0, a[lo:lo + BAND, :BAND], 0.0)], axis=0)
    own = jnp.where(c == 0, own, 0.0)
    summed = comm.psum(own.reshape(rows * cols, -1, 128), ("row", "col"), rows * cols)
    summed = summed.reshape(2 * BAND, BAND)
    gram0, top0 = summed[:BAND], summed[BAND:]
    colb = comm.broadcast(a[:, :width], "col", cols, 0)
    p0 = jnp.where(row_pos[:, None] >= lo, colb[:, :BAND], 0.0)
    strip_t = strip.T

    stored = []
    current = a
    prev = None
    for k in range(PANELS):
        lo = (k + 1) * BAND
        if k == 0:
            gram, top = gram0, top0
            pr = p0
            pc = jnp.where(col_pos[:, None] >= lo, strip_t[:, :BAND], 0.0)
        else:
            y_r0, w_r0, y_c0, w_c0, y_e0, w_e0 = prev
            pr = colb[:, k * BAND:(k + 1) * BAND] - mm_nt(y_r0, w_e0) - mm_nt(w_r0, y_e0)
            pc = strip_t[:, k * BAND:(k + 1) * BAND] - mm_nt(y_c0, w_e0) - mm_nt(w_c0, y_e0)
            pr = jnp.where(row_pos[:, None] >= lo, pr, 0.0)
            pc = jnp.where(col_pos[:, None] >= lo, pc, 0.0)
            top_part = jnp.where(c == 0, pc[lo:lo + BAND], 0.0)
            summed = comm.psum(jnp.concatenate([mm_tn(pc, pc), top_part], axis=0), "col", cols)
            gram, top = summed[:BAND], summed[BAND:]
        low_inv, transform = small_factors(gram, top)
        unit_r = (row_pos[:, None] - lo == band_idx[None, :]).astype(jnp.float32)
        unit_c = (col_pos[:, None] - lo == band_idx[None, :]).astype(jnp.float32)
        y_r = mm_nt(pr, low_inv) + unit_r
        y_c = mm_nt(pc, low_inv) + unit_c
        stored.append(y_r)

        xp = mm(current, y_c, FAST)
        xq = mm_tn(current, y_r, FAST)
        summed_c = comm.psum(jnp.concatenate([xq, mm_tn(y_r, xp)], axis=0), "row", rows)
        x_c = summed_c[:col_count]
        parts = [xp, summed_c[col_count:]]
        if k + 1 < PANELS:
            nlo = (k + 1) * BAND
            parts.append(mm_tn(strip_t[:, nlo:nlo + BAND], y_c))
        summed = comm.psum(jnp.concatenate(parts, axis=0), "col", cols)
        x_r = summed[:row_count]
        curv = summed[row_count:row_count + BAND]
        middle = mm_nt(mm(transform, curv), transform)
        w_r = mm_nt(x_r, transform) - 0.5 * mm(y_r, middle)
        w_c = mm_nt(x_c, transform) - 0.5 * mm(y_c, middle)
        current = current - mm_nt(y_r, w_c, FAST) - mm_nt(w_r, y_c, FAST)
        if k + 1 < PANELS:
            x_e = summed[row_count + BAND:]
            y_e = mm_nt(top, low_inv) + jnp.eye(BAND, dtype=jnp.float32)
            w_e = mm_nt(x_e, transform) - 0.5 * mm(y_e, middle)
            prev = (y_r, w_r, y_c, w_c, y_e, w_e)
    return current, jnp.concatenate(stored, axis=1)


def solution(mesh):
    return jax.shard_map(
        body,
        mesh=mesh,
        in_specs=(P("row", "col"),),
        out_specs=(P("row", "col"), P("row", None)),
        check_vma=False,
    )
```

```python
import jax
import jax.numpy as jnp
from jax import lax
from jax.sharding import PartitionSpec as P

BAND = 256
PANELS = 2
HIGH = lax.Precision.HIGH
FAST = lax.Precision.HIGH


def mm(a, b, precision=HIGH):
    return jnp.dot(a, b, precision=precision)


def mm_tn(a, b, precision=HIGH):
    return lax.dot_general(a, b, (((0,), (0,)), ((), ())), precision=precision)


def mm_nt(a, b, precision=HIGH):
    return lax.dot_general(a, b, (((1,), (1,)), ((), ())), precision=precision)


class Comm:
    def a2a(self, x, axis):
        return lax.all_to_all(x, axis, 0, 0, tiled=False)

    def reduce_scatter(self, x, axis, groups):
        parts = self.a2a(x.reshape(groups, x.shape[0] // groups, *x.shape[1:]), axis)
        return jnp.sum(parts, axis=0)

    def all_gather(self, x, axis, groups):
        got = self.a2a(jnp.broadcast_to(x[None], (groups,) + x.shape), axis)
        return got.reshape(groups * x.shape[0], *x.shape[1:])

    def psum(self, x, axis, groups):
        return self.all_gather(self.reduce_scatter(x, axis, groups), axis, groups)

    def broadcast(self, x, axis, groups, root):
        parts = self.a2a(x.reshape(groups, x.shape[0] // groups, *x.shape[1:]), axis)
        return self.all_gather(parts[root], axis, groups)


def transpose_exchange(x, rows, cols):
    both = ("row", "col")
    first = []
    second = []
    for s in range(rows):
        for j in range(cols):
            src = s * cols + j
            first.append((src, (2 * j + s % 2) * cols + s // 2))
            second.append((src, (2 * j + 1 - s % 2) * cols + s // 2))
    got1 = lax.ppermute(x, both, first)
    got2 = lax.ppermute(x, both, second)
    odd_row = lax.axis_index("row") % 2 == 1
    even = jnp.where(odd_row, got2, got1)
    odd = jnp.where(odd_row, got1, got2)
    return jnp.concatenate([even, odd], axis=0)


def cholesky_inverse(spd):
    half = spd.shape[0] // 2
    identity = jnp.eye(half, dtype=spd.dtype)
    low11 = jnp.linalg.cholesky(spd[:half, :half])
    inv11 = jax.scipy.linalg.solve_triangular(low11, identity, lower=True)
    low21 = mm_nt(spd[half:, :half], inv11)
    low22 = jnp.linalg.cholesky(spd[half:, half:] - mm_nt(low21, low21))
    inv22 = jax.scipy.linalg.solve_triangular(low22, identity, lower=True)
    inv21 = -mm(mm(inv22, low21), inv11)
    upper = jnp.concatenate([inv11, jnp.zeros_like(inv11)], axis=1)
    lower = jnp.concatenate([inv21, inv22], axis=1)
    return jnp.concatenate([upper, lower], axis=0)


def small_factors(gram, top):
    identity = jnp.eye(BAND, dtype=jnp.float32)
    low_inv = cholesky_inverse(gram)
    shifted = identity + mm_nt(top, low_inv)
    second_inv = cholesky_inverse(mm_nt(shifted, shifted))
    transform = mm_tn(shifted, mm_tn(second_inv, second_inv))
    return low_inv, transform


def body(a):
    comm = Comm()
    rows = lax.psum(1, "row")
    cols = lax.psum(1, "col")
    row_count, col_count = a.shape
    r = lax.axis_index("row")
    c = lax.axis_index("col")
    row_pos = r * row_count + jnp.arange(row_count, dtype=jnp.int32)
    col_pos = c * col_count + jnp.arange(col_count, dtype=jnp.int32)
    band_idx = jnp.arange(BAND, dtype=jnp.int32)
    width = PANELS * BAND

    strip = lax.psum(jnp.where(r == 0, a[:width, :], 0.0), "row")
    lo = BAND
    p0_own = jnp.where(row_pos[:, None] >= lo, a[:, :BAND], 0.0)
    own = jnp.concatenate([mm_tn(p0_own, p0_own), jnp.where(r == 0, a[lo:lo + BAND, :BAND], 0.0)], axis=0)
    own = jnp.where(c == 0, own, 0.0)
    summed = comm.psum(own.reshape(rows * cols, -1, 128), ("row", "col"), rows * cols)
    summed = summed.reshape(2 * BAND, BAND)
    gram0, top0 = summed[:BAND], summed[BAND:]
    colb = comm.broadcast(a[:, :width], "col", cols, 0)
    p0 = jnp.where(row_pos[:, None] >= lo, colb[:, :BAND], 0.0)
    strip_t = strip.T

    stored = []
    current = a
    prev = None
    for k in range(PANELS):
        lo = (k + 1) * BAND
        if k == 0:
            gram, top = gram0, top0
            pr = p0
            pc = jnp.where(col_pos[:, None] >= lo, strip_t[:, :BAND], 0.0)
        else:
            y_r0, w_r0, y_c0, w_c0, y_e0, w_e0 = prev
            pr = colb[:, k * BAND:(k + 1) * BAND] - mm_nt(y_r0, w_e0) - mm_nt(w_r0, y_e0)
            pc = strip_t[:, k * BAND:(k + 1) * BAND] - mm_nt(y_c0, w_e0) - mm_nt(w_c0, y_e0)
            pr = jnp.where(row_pos[:, None] >= lo, pr, 0.0)
            pc = jnp.where(col_pos[:, None] >= lo, pc, 0.0)
            top_part = jnp.where(c == 0, pc[lo:lo + BAND], 0.0)
            summed = comm.psum(jnp.concatenate([mm_tn(pc, pc), top_part], axis=0), "col", cols)
            gram, top = summed[:BAND], summed[BAND:]
        low_inv, transform = small_factors(gram, top)
        if k == 0:
            low_inv, transform = lax.optimization_barrier((low_inv, transform))
        unit_r = (row_pos[:, None] - lo == band_idx[None, :]).astype(jnp.float32)
        unit_c = (col_pos[:, None] - lo == band_idx[None, :]).astype(jnp.float32)
        y_r = mm_nt(pr, low_inv) + unit_r
        y_c = mm_nt(pc, low_inv) + unit_c
        stored.append(y_r)

        xp = mm(current, y_c, FAST)
        xq = mm_tn(current, y_r, FAST)
        summed_c = comm.psum(jnp.concatenate([xq, mm_tn(y_r, xp)], axis=0), "row", rows)
        x_c = summed_c[:col_count]
        parts = [xp, summed_c[col_count:]]
        if k + 1 < PANELS:
            nlo = (k + 1) * BAND
            parts.append(mm_tn(strip_t[:, nlo:nlo + BAND], y_c))
        summed = comm.psum(jnp.concatenate(parts, axis=0), "col", cols)
        x_r = summed[:row_count]
        curv = summed[row_count:row_count + BAND]
        middle = mm_nt(mm(transform, curv), transform)
        w_r = mm_nt(x_r, transform) - 0.5 * mm(y_r, middle)
        w_c = mm_nt(x_c, transform) - 0.5 * mm(y_c, middle)
        current = current - mm_nt(y_r, w_c, FAST) - mm_nt(w_r, y_c, FAST)
        if k + 1 < PANELS:
            x_e = summed[row_count + BAND:]
            y_e = mm_nt(top, low_inv) + jnp.eye(BAND, dtype=jnp.float32)
            w_e = mm_nt(x_e, transform) - 0.5 * mm(y_e, middle)
            prev = (y_r, w_r, y_c, w_c, y_e, w_e)
    return current, jnp.concatenate(stored, axis=1)


def solution(mesh):
    return jax.shard_map(
        body,
        mesh=mesh,
        in_specs=(P("row", "col"),),
        out_specs=(P("row", "col"), P("row", None)),
        check_vma=False,
    )
```

```python
import jax
import jax.numpy as jnp
from jax import lax
from jax.sharding import PartitionSpec as P

BAND = 256
PANELS = 2
HIGH = lax.Precision.HIGH
FAST = lax.Precision.HIGH


def mm(a, b, precision=HIGH):
    return jnp.dot(a, b, precision=precision)


def mm_tn(a, b, precision=HIGH):
    return lax.dot_general(a, b, (((0,), (0,)), ((), ())), precision=precision)


def mm_nt(a, b, precision=HIGH):
    return lax.dot_general(a, b, (((1,), (1,)), ((), ())), precision=precision)


class Comm:
    def a2a(self, x, axis):
        return lax.all_to_all(x, axis, 0, 0, tiled=False)

    def reduce_scatter(self, x, axis, groups):
        parts = self.a2a(x.reshape(groups, x.shape[0] // groups, *x.shape[1:]), axis)
        return jnp.sum(parts, axis=0)

    def all_gather(self, x, axis, groups):
        got = self.a2a(jnp.broadcast_to(x[None], (groups,) + x.shape), axis)
        return got.reshape(groups * x.shape[0], *x.shape[1:])

    def psum(self, x, axis, groups):
        return self.all_gather(self.reduce_scatter(x, axis, groups), axis, groups)

    def broadcast(self, x, axis, groups, root):
        parts = self.a2a(x.reshape(groups, x.shape[0] // groups, *x.shape[1:]), axis)
        return self.all_gather(parts[root], axis, groups)


def transpose_exchange(x, rows, cols):
    both = ("row", "col")
    first = []
    second = []
    for s in range(rows):
        for j in range(cols):
            src = s * cols + j
            first.append((src, (2 * j + s % 2) * cols + s // 2))
            second.append((src, (2 * j + 1 - s % 2) * cols + s // 2))
    got1 = lax.ppermute(x, both, first)
    got2 = lax.ppermute(x, both, second)
    odd_row = lax.axis_index("row") % 2 == 1
    even = jnp.where(odd_row, got2, got1)
    odd = jnp.where(odd_row, got1, got2)
    return jnp.concatenate([even, odd], axis=0)


def cholesky_inverse(spd):
    half = spd.shape[0] // 2
    identity = jnp.eye(half, dtype=spd.dtype)
    low11 = jnp.linalg.cholesky(spd[:half, :half])
    inv11 = jax.scipy.linalg.solve_triangular(low11, identity, lower=True)
    low21 = mm_nt(spd[half:, :half], inv11)
    low22 = jnp.linalg.cholesky(spd[half:, half:] - mm_nt(low21, low21))
    inv22 = jax.scipy.linalg.solve_triangular(low22, identity, lower=True)
    inv21 = -mm(mm(inv22, low21), inv11)
    upper = jnp.concatenate([inv11, jnp.zeros_like(inv11)], axis=1)
    lower = jnp.concatenate([inv21, inv22], axis=1)
    return jnp.concatenate([upper, lower], axis=0)


def small_factors(gram, top):
    identity = jnp.eye(BAND, dtype=jnp.float32)
    low_inv = cholesky_inverse(gram)
    shifted = identity + mm_nt(top, low_inv)
    second_inv = cholesky_inverse(mm_nt(shifted, shifted))
    transform = mm_tn(shifted, mm_tn(second_inv, second_inv))
    return low_inv, transform


def body(a):
    comm = Comm()
    rows = lax.psum(1, "row")
    cols = lax.psum(1, "col")
    row_count, col_count = a.shape
    r = lax.axis_index("row")
    c = lax.axis_index("col")
    row_pos = r * row_count + jnp.arange(row_count, dtype=jnp.int32)
    col_pos = c * col_count + jnp.arange(col_count, dtype=jnp.int32)
    band_idx = jnp.arange(BAND, dtype=jnp.int32)
    width = PANELS * BAND

    strip = lax.psum(jnp.where(r == 0, a[:width, :], 0.0), "row")
    lo = BAND
    p0_own = jnp.where(row_pos[:, None] >= lo, a[:, :BAND], 0.0)
    own = jnp.concatenate([mm_tn(p0_own, p0_own), jnp.where(r == 0, a[lo:lo + BAND, :BAND], 0.0)], axis=0)
    own = jnp.where(c == 0, own, 0.0)
    summed = comm.psum(own.reshape(rows * cols, -1, 128), ("row", "col"), rows * cols)
    summed = summed.reshape(2 * BAND, BAND)
    gram0, top0 = summed[:BAND], summed[BAND:]
    colb = comm.broadcast(a[:, :width], "col", cols, 0)
    p0 = jnp.where(row_pos[:, None] >= lo, colb[:, :BAND], 0.0)
    strip_t = strip.T

    stored = []
    current = a
    prev = None
    for k in range(PANELS):
        lo = (k + 1) * BAND
        if k == 0:
            gram, top = gram0, top0
            pr = p0
            pc = jnp.where(col_pos[:, None] >= lo, strip_t[:, :BAND], 0.0)
        else:
            y_r0, w_r0, y_c0, w_c0, y_e0, w_e0 = prev
            pr = colb[:, k * BAND:(k + 1) * BAND] - mm_nt(y_r0, w_e0) - mm_nt(w_r0, y_e0)
            pc = strip_t[:, k * BAND:(k + 1) * BAND] - mm_nt(y_c0, w_e0) - mm_nt(w_c0, y_e0)
            pr = jnp.where(row_pos[:, None] >= lo, pr, 0.0)
            pc = jnp.where(col_pos[:, None] >= lo, pc, 0.0)
            top_part = jnp.where(c == 0, pc[lo:lo + BAND], 0.0)
            summed = comm.psum(jnp.concatenate([mm_tn(pc, pc), top_part], axis=0), "col", cols)
            gram, top = summed[:BAND], summed[BAND:]
        low_inv, transform = small_factors(gram, top)
        if k == 0:
            low_inv, transform = lax.optimization_barrier((low_inv, transform))
        unit_r = (row_pos[:, None] - lo == band_idx[None, :]).astype(jnp.float32)
        unit_c = (col_pos[:, None] - lo == band_idx[None, :]).astype(jnp.float32)
        y_r = mm_nt(pr, low_inv) + unit_r
        y_c = mm_nt(pc, low_inv) + unit_c
        stored.append(y_r)

        xp = mm(current, y_c, FAST)
        xq = mm_tn(current, y_r, FAST)
        x_c = comm.psum(xq, "row", rows)
        parts = [xp]
        if k + 1 < PANELS:
            nlo = (k + 1) * BAND
            parts.append(mm_tn(strip_t[:, nlo:nlo + BAND], y_c))
        summed = comm.psum(jnp.concatenate(parts, axis=0), "col", cols)
        x_r = summed[:row_count]
        curv = comm.psum(mm_tn(y_c, x_c), "col", cols)
        middle = mm_nt(mm(transform, curv), transform)
        w_r = mm_nt(x_r, transform) - 0.5 * mm(y_r, middle)
        w_c = mm_nt(x_c, transform) - 0.5 * mm(y_c, middle)
        current = current - mm_nt(y_r, w_c, FAST) - mm_nt(w_r, y_c, FAST)
        if k + 1 < PANELS:
            x_e = summed[row_count:]
            y_e = mm_nt(top, low_inv) + jnp.eye(BAND, dtype=jnp.float32)
            w_e = mm_nt(x_e, transform) - 0.5 * mm(y_e, middle)
            prev = (y_r, w_r, y_c, w_c, y_e, w_e)
    return current, jnp.concatenate(stored, axis=1)


def solution(mesh):
    return jax.shard_map(
        body,
        mesh=mesh,
        in_specs=(P("row", "col"),),
        out_specs=(P("row", "col"), P("row", None)),
        check_vma=False,
    )
```
